32 devices in a mesh: groups: 2 (over x), section: 8 (over z, y), sub: 2 (over core).
Axes of the slice: x: 2, y: 2, z: 4, core: 2. Of those that a mesh axis runs over, the one named last changes fastest.
Arguments:
- voltages: bfloat16 [2048, 2, 65920], P(('groups', 'section', 'sub')), parts along dimension 0, may hold values from -6 to 6
- prototype: float32 [512], replicated, may hold values from 0.02 to 0.07
- beam_weights: bfloat16 [256, 2, 1024, 1024], P(('groups', 'section', 'sub')), parts along dimension 0, may hold values from -0.125 to 0.125
- input_order: int32 [1024], replicated, may hold values from 0 to 1023, each once
- beam_order: int32 [1024], replicated, may hold values from 0 to 1023, each once
- trial_delays: int32 [256, 128], replicated, may hold values from 0 to 127, as said below
Outputs:
- dedispersed: float32 [256, 2048, 128], P(None, ('groups', 'section', 'sub')), parts along dimension 1
The draws below stay inside these ranges and needn't reach their ends.
There are 2 independent parts, one for each index of `groups`. The reference program is written for one: setup_inputs(seed, part) draws one part's arguments, and reference() takes and returns one part's arrays. A program takes and returns all parts, laid end to end along the dimension named above; an argument that names none is the same for every part. Nothing has to cross between parts.
Inputs may be any that keep to these rules, and one draw needn't show every extreme that they name: `input_order`: each physical input appears once. `beam_order`: each physical beam appears once. `trial_delays`: for each trial the delays do not rise with the channel index.
All inputs are finite; a program needn't handle non-finite values.
Results may differ from the reference program's by a relative error of at most 0.0043.
Values may be sent and summed in bfloat16 or wider, within the bound.
No kernel may reach another device: no remote copies, remote signals or barrier semaphores. Data moves between devices by JAX's collectives and lax.ppermute only.
A program may use at most 256 MiB of HBM per device.

```python
import math
import jax
import jax.numpy as jnp
from jax import lax

CHANS = 128
INPUTS = 1024
BEAMS = 1024
TRIALS = 256
TAPS = 4
DOWN = 4
SPECTRA = 512
BINS = 128
RAW_LEN = 65920


def draw_trial_delays(key, part):
    top_key = jax.random.fold_in(key, 7)
    value_key = jax.random.fold_in(key, 11)
    top_values = jax.random.randint(top_key, (TRIALS,), BINS // 4, BINS, dtype=jnp.int32)
    top_values = top_values.at[0].set(BINS - 1)
    raw_values = jax.random.randint(value_key, (TRIALS, CHANS), 0, top_values[:, None] + 1, dtype=jnp.int32)
    ordered = -jnp.sort(-raw_values, axis=1)
    ordered = ordered.at[0, 0].set(BINS - 1)
    ordered = ordered.at[0, CHANS - 1].set(0)
    return ordered


def steps_of(rng, extent, cuts, smallest, largest):
    loudness, own = 1.0, jax.random.fold_in(rng, 6)
    for dim, parts in cuts:
        steps = jnp.exp(jax.random.uniform(jax.random.fold_in(own, dim), (parts,), jnp.float32, smallest / len(cuts), largest / len(cuts)))
        loudness = loudness * jnp.repeat(steps, extent[dim] // parts).reshape([-1 if axis == dim else 1 for axis in range(len(extent))])
    return loudness


def scatter_about(own_key, dims, width, most, split=(), held_as=jnp.bfloat16):
    values = width * jax.random.normal(own_key, dims, jnp.float32)
    if split:
        values = values * steps_of(own_key, dims, split, -0.22, 0.18)
    return jnp.clip(values, -most, most).astype(held_as)


def setup_inputs(seed: int = 0, part: int = 0) -> dict:
    keys = jax.random.split(jax.random.key(seed), 7)
    part_splits = jax.random.split(jax.random.fold_in(keys[6], part), 7)
    return {
        "voltages": scatter_about(part_splits[0], (INPUTS, 2, RAW_LEN), 1.0, 6.0, ((0, 16),)),
        "prototype": jnp.clip(jax.random.uniform(keys[1], (TAPS * CHANS,), jnp.float32, 0.02, 0.07), 0.02, 0.07),
        "beam_weights": scatter_about(part_splits[2], (CHANS, 2, BEAMS, INPUTS), (2 * INPUTS) ** -0.5, 0.125, ((0, 16),)),
        "input_order": jax.random.permutation(keys[3], INPUTS).astype(jnp.int32),
        "beam_order": jax.random.permutation(keys[4], BEAMS).astype(jnp.int32),
        "trial_delays": draw_trial_delays(jax.random.fold_in(keys[6], 71), part),
    }


def filter_matrix(prototype):
    channel_index = jnp.arange(CHANS, dtype=jnp.int32)
    phase_step = channel_index[:, None] * channel_index[None, :] % CHANS
    angles = 2.0 * math.pi / CHANS * phase_step.astype(jnp.float32)
    cosine = jnp.tile(jnp.cos(angles), (1, TAPS)) * prototype[None, :]
    sine_part = jnp.tile(jnp.sin(angles), (1, TAPS)) * prototype[None, :]
    real_rows = jnp.concatenate([cosine, sine_part], axis=1)
    imag_rows = jnp.concatenate([-sine_part, cosine], axis=1)
    return jnp.stack([real_rows, imag_rows], axis=0).astype(jnp.bfloat16)

def channelize(block_volts, matrix):
    input_count = block_volts.shape[0]
    frames = block_volts.reshape(input_count, 2, SPECTRA + TAPS - 1, CHANS)
    windows = jnp.concatenate([frames[:, part_index, tap_index:tap_index + SPECTRA, :] for part_index in range(2) for tap_index in range(TAPS)], axis=2)
    result = lax.dot_general(matrix.astype(jnp.float32), windows.astype(jnp.float32), (((2,), (2,)), ((), ())), preferred_element_type=jnp.float32)
    return result.astype(jnp.bfloat16)

def reference(voltages, prototype, beam_weights, input_order, beam_order, trial_delays):
    matrix = filter_matrix(prototype)
    grouped = voltages.reshape(INPUTS // 8, 8, 2, RAW_LEN)

    def channelize_block(block_volts):
        return channelize(block_volts, matrix)
    pieces = lax.map(channelize_block, grouped)
    channelized = jnp.transpose(pieces, (2, 1, 0, 3, 4)).reshape(CHANS, 2, INPUTS, SPECTRA)

    def one_channel(operands):
        weights_here, volts_here = operands
        picked = jnp.take(jnp.take(weights_here, beam_order, axis=1), input_order, axis=2)
        beam_real = jnp.dot(picked[0], volts_here[0], preferred_element_type=jnp.float32) - jnp.dot(picked[1], volts_here[1], preferred_element_type=jnp.float32)
        beam_imag = jnp.dot(picked[0], volts_here[1], preferred_element_type=jnp.float32) + jnp.dot(picked[1], volts_here[0], preferred_element_type=jnp.float32)
        power = beam_real * beam_real + beam_imag * beam_imag
        return power.reshape(BEAMS, BINS, DOWN).sum(axis=2)
    folded = lax.map(one_channel, (beam_weights, channelized))
    centred = folded - lax.optimization_barrier(jnp.mean(folded, axis=2, keepdims=True))
    spread = lax.optimization_barrier(jnp.mean(centred * centred, axis=2, keepdims=True))
    normed = centred / jnp.sqrt(spread + 1e-06)
    sample_index = jnp.arange(BINS, dtype=jnp.int32)

    def one_trial(delays):
        row_map = (sample_index[None, :] + delays[:, None].astype(jnp.int32)) % BINS
        shifted = jnp.take_along_axis(normed, jnp.broadcast_to(row_map[:, None, :], normed.shape), axis=2)
        return lax.optimization_barrier(jnp.sum(shifted, axis=0)) / math.sqrt(CHANS)
    return lax.map(one_trial, trial_delays)
```

```python
import math

import jax
import jax.numpy as jnp
from jax import lax
from jax.experimental import pallas as pl
from jax.experimental.pallas import tpu as pltpu
from jax.sharding import PartitionSpec as P

CHANS = 128
INPUTS = 1024
BEAMS = 1024
TAPS = 4
DOWN = 4
SPECTRA = 512
BINS = 128
LANES = 128
OWNER_AXES = ("section", "sub")
VMEM_LIMIT = 56 << 20
U_BLOCK = 16
TRIAL_BLOCK = 16
FREQS = BINS // 2 + 1
FREQ_ROWS = 80
FREQ_BLOCK = 5
BEAM_BLOCK = 256


def filter_matrix(prototype):
    channel_index = jnp.arange(CHANS, dtype=jnp.int32)
    phase_step = channel_index[:, None] * channel_index[None, :] % CHANS
    angles = 2.0 * math.pi / CHANS * phase_step.astype(jnp.float32)
    cosine = jnp.tile(jnp.cos(angles), (1, TAPS)) * prototype[None, :]
    sine_part = jnp.tile(jnp.sin(angles), (1, TAPS)) * prototype[None, :]
    real_rows = jnp.concatenate([cosine, sine_part], axis=1)
    imag_rows = jnp.concatenate([-sine_part, cosine], axis=1)
    return jnp.stack([real_rows, imag_rows], axis=0).astype(jnp.bfloat16)


def channelize_kernel(owners, count, main_ref, *refs):
    halo_refs = refs[: TAPS - 1]
    bank_ref, out_ref, turned, spread = refs[TAPS - 1 :]
    rows = owners * count
    block = U_BLOCK * DOWN
    half = main_ref.shape[0] // 2

    def turn(step, carry):
        start = pl.multiple_of(step * LANES, LANES)
        turned[pl.ds(start, LANES), :] = main_ref[:, pl.ds(start, LANES)].T
        return carry

    lax.fori_loop(0, block, turn, 0, unroll=4)
    for tap in range(TAPS - 1):
        turned[(block + tap) * LANES : (block + tap + 1) * LANES, :] = halo_refs[tap][...].T
    lane = lax.broadcasted_iota(jnp.int32, (rows, LANES), 1)
    sign = jnp.where(lane < half, 1.0, -1.0).astype(jnp.float32)

    def spectra(u, carry):
        for pair in range(DOWN // 2):
            base = u * DOWN + pair * 2
            pieces = [
                turned[pl.ds(pl.multiple_of((base + e) * LANES, LANES), TAPS * LANES), :]
                for e in range(2)
            ]
            both = jnp.dot(
                bank_ref[...],
                jnp.concatenate(pieces, axis=1),
                preferred_element_type=jnp.float32,
            )
            for e in range(2):
                own = both[:rows, e * LANES : (e + 1) * LANES]
                other = both[rows:, e * LANES : (e + 1) * LANES]
                value = own + sign * pltpu.roll(other, half, axis=1)
                m = pair * 2 + e
                spread[pl.ds(m * U_BLOCK + u, rows, stride=block), :] = value
        return carry

    lax.fori_loop(0, U_BLOCK, spectra, 0, unroll=2)
    out_ref[...] = spread[...].reshape(out_ref.shape).astype(jnp.bfloat16)


def channelize_chunk(turned_volts, bank, owners, count):
    width = turned_volts.shape[0]
    block = U_BLOCK * DOWN
    steps = SPECTRA // block
    rows = owners * count
    return pl.pallas_call(
        lambda *refs: channelize_kernel(owners, count, *refs),
        out_shape=jax.ShapeDtypeStruct((owners, count, DOWN, BINS, width), jnp.bfloat16),
        grid=(steps,),
        in_specs=[pl.BlockSpec((width, block * LANES), lambda g: (0, g))]
        + [
            pl.BlockSpec((width, LANES), lambda g, tap=tap: (0, (g + 1) * block + tap))
            for tap in range(TAPS - 1)
        ]
        + [pl.BlockSpec((2 * rows, TAPS * LANES), lambda g: (0, 0))],
        out_specs=pl.BlockSpec((owners, count, DOWN, U_BLOCK, width), lambda g: (0, 0, 0, g, 0)),
        scratch_shapes=[
            pltpu.VMEM(((block + TAPS - 1) * LANES, LANES), jnp.bfloat16),
            pltpu.VMEM((rows * block, LANES), jnp.float32),
        ],
        compiler_params=pltpu.CompilerParams(vmem_limit_bytes=VMEM_LIMIT),
        cost_estimate=pl.CostEstimate(
            flops=2 * 2 * CHANS * width * SPECTRA * TAPS * LANES,
            bytes_accessed=turned_volts.size * 2 + rows * SPECTRA * width * 2,
            transcendentals=0,
        ),
        name="channelize",
    )(turned_volts, *([turned_volts] * (TAPS - 1)), bank)


def beam_kernel(sources, arrived_ref, weight_ref, pick_ref, out_ref, normed):
    tile = pl.program_id(1)
    inputs = weight_ref.shape[2]
    part = inputs // sources
    spectra = jnp.concatenate([arrived_ref[s, 0] for s in range(sources)], axis=1)
    first = weight_ref[0, 0]
    second = weight_ref[0, 1]
    negative = -second
    real_rows = []
    imag_rows = []
    for s in range(sources):
        rows = slice(s * part, (s + 1) * part)
        real_rows += [first[rows], negative[rows]]
        imag_rows += [second[rows], first[rows]]
    beam_real = jnp.dot(
        spectra, jnp.concatenate(real_rows, axis=0), preferred_element_type=jnp.float32
    )
    beam_imag = jnp.dot(
        spectra, jnp.concatenate(imag_rows, axis=0), preferred_element_type=jnp.float32
    )
    power = beam_real * beam_real + beam_imag * beam_imag
    folded = power[:BINS]
    for m in range(1, DOWN):
        folded = folded + power[m * BINS : (m + 1) * BINS]
    centred = folded - jnp.mean(folded, axis=0, keepdims=True)
    spread = jnp.mean(centred * centred, axis=0, keepdims=True)
    start = pl.multiple_of(tile * BEAM_BLOCK, BEAM_BLOCK)
    normed[:, pl.ds(start, BEAM_BLOCK)] = (centred / jnp.sqrt(spread + 1e-06)).astype(jnp.bfloat16)

    @pl.when(tile == pl.num_programs(1) - 1)
    def _():
        picked = lax.dot_general(
            pick_ref[...],
            normed[...],
            (((1,), (1,)), ((), ())),
            preferred_element_type=jnp.float32,
        )
        out_ref[...] = picked.astype(jnp.bfloat16).reshape(out_ref.shape)


def beam_chunk(arrived, weights, pick, owners):
    sources, count, spectra, width = arrived.shape
    _, _, inputs, beams = weights.shape
    return pl.pallas_call(
        lambda *refs: beam_kernel(sources, *refs),
        out_shape=jax.ShapeDtypeStruct((owners, count, beams // owners, BINS), jnp.bfloat16),
        grid=(count, beams // BEAM_BLOCK),
        in_specs=[
            pl.BlockSpec((sources, 1, spectra, width), lambda c, b: (0, c, 0, 0)),
            pl.BlockSpec((1, 2, inputs, BEAM_BLOCK), lambda c, b: (c, 0, 0, b)),
            pl.BlockSpec((beams, beams), lambda c, b: (0, 0)),
        ],
        out_specs=pl.BlockSpec((owners, 1, beams // owners, BINS), lambda c, b: (0, c, 0, 0)),
        scratch_shapes=[pltpu.VMEM((BINS, beams), jnp.bfloat16)],
        compiler_params=pltpu.CompilerParams(vmem_limit_bytes=VMEM_LIMIT),
        cost_estimate=pl.CostEstimate(
            flops=count * 8 * spectra * inputs * beams,
            bytes_accessed=arrived.size * 2 + weights.size * 2,
            transcendentals=0,
        ),
        name="beamform",
    )(arrived, weights, pick)


def split_parts(values):
    high = lax.reduce_precision(values, 8, 7)
    return high.astype(jnp.bfloat16), (values - high).astype(jnp.bfloat16)


def forward_table():
    freq = jnp.arange(FREQ_ROWS, dtype=jnp.int32)
    sample = jnp.arange(BINS, dtype=jnp.int32)
    angles = (2.0 * math.pi / BINS) * (freq[:, None] * sample[None, :] % BINS).astype(jnp.float32)
    used = (freq < FREQS)[:, None]
    rows = jnp.concatenate(
        [jnp.where(used, jnp.cos(angles), 0.0), jnp.where(used, -jnp.sin(angles), 0.0)], axis=0
    )
    return jnp.concatenate(split_parts(rows), axis=1)


def inverse_table():
    freq = jnp.arange(FREQ_ROWS, dtype=jnp.int32)
    sample = jnp.arange(BINS, dtype=jnp.int32)
    angles = (2.0 * math.pi / BINS) * (sample[:, None] * freq[None, :] % BINS).astype(jnp.float32)
    edge = (freq == 0) | (freq == BINS // 2)
    weight = jnp.where(freq < FREQS, jnp.where(edge, 1.0, 2.0), 0.0)
    weight = weight / (BINS * math.sqrt(CHANS))
    rows = jnp.concatenate([jnp.cos(angles) * weight, -jnp.sin(angles) * weight], axis=0)
    high, low = split_parts(rows)
    return jnp.concatenate([high, high, low], axis=1)


def phase_table(delays):
    freq = jnp.arange(FREQS, dtype=jnp.int32)
    index = freq[:, None, None] * delays[None] % BINS
    angles = (2.0 * math.pi / BINS) * index.astype(jnp.float32)
    both = jnp.concatenate([jnp.cos(angles), jnp.sin(angles)], axis=2)
    return jnp.concatenate(split_parts(both), axis=2)


def split_inside(values):
    high = values.astype(jnp.bfloat16)
    return high, (values - high.astype(jnp.float32)).astype(jnp.bfloat16)


def dedisperse_kernel(pieces, channels, trials, freq_steps, *refs):
    series_refs = refs[:pieces]
    phase_ref, forward_ref, inverse_ref, out_ref, spec, turned = refs[pieces:]
    step = pl.program_id(0)
    half = LANES // 2

    def low_lanes(rows):
        return lax.broadcasted_iota(jnp.int32, (rows, LANES), 1) < half

    @pl.when(step == 0)
    def _():
        low = low_lanes(FREQ_ROWS)
        tail = 16
        for d in range(trials):
            turned[(d + 1) * FREQ_ROWS - tail : (d + 1) * FREQ_ROWS, :] = jnp.zeros(
                (tail, LANES), jnp.float32
            )
        base = 0
        for ref in series_refs:
            pairs = ref.shape[0]

            def one_pair(pair, carry, ref=ref, base=base):
                both = ref[pair]
                result = lax.dot_general(
                    forward_ref[...],
                    jnp.concatenate([both, both], axis=1),
                    (((1,), (1,)), ((), ())),
                    preferred_element_type=jnp.float32,
                )
                real, imag = result[:FREQ_ROWS], result[FREQ_ROWS:]
                even = jnp.where(low, real, pltpu.roll(imag, half, axis=1))
                odd = jnp.where(low, pltpu.roll(real, half, axis=1), imag)
                channel = base + 2 * pair
                spec[pl.ds(channel, FREQ_ROWS, stride=channels), :] = even
                spec[pl.ds(channel + 1, FREQ_ROWS, stride=channels), :] = odd
                return carry

            lax.fori_loop(0, pairs, one_pair, 0, unroll=2)
            base += 2 * pairs

    @pl.when(step < freq_steps)
    def _():
        sign = jnp.where(low_lanes(channels), -1.0, 1.0).astype(jnp.float32)
        for local in range(FREQ_BLOCK):
            freq = step * FREQ_BLOCK + local
            own = spec[pl.ds(pl.multiple_of(freq * channels, channels), channels), :]
            full = jnp.concatenate([own, sign * pltpu.roll(own, half, axis=1)], axis=0)
            high, low = split_inside(full)
            phase = phase_ref[local]
            result = jnp.dot(
                jnp.concatenate([phase, phase[:, : 2 * channels]], axis=1),
                jnp.concatenate([high, high, low], axis=0),
                preferred_element_type=jnp.float32,
            )
            turned[pl.ds(freq, trials, stride=FREQ_ROWS), :] = result

    @pl.when(step >= freq_steps)
    def _():
        low_half = low_lanes(BINS)

        def one_pair(pair, carry):
            columns = []
            for e in range(2):
                trial = (step - freq_steps) * TRIAL_BLOCK + 2 * pair + e
                start = pl.multiple_of(trial * FREQ_ROWS, FREQ_ROWS)
                high, low = split_inside(turned[pl.ds(start, FREQ_ROWS), :])
                columns.append(jnp.concatenate([high, low, high], axis=0))
            result = jnp.dot(
                inverse_ref[...],
                jnp.concatenate(columns, axis=1),
                preferred_element_type=jnp.float32,
            )
            first = result[:BINS, :LANES] + pltpu.roll(result[BINS:, :LANES], half, axis=1)
            second = pltpu.roll(result[:BINS, LANES:], half, axis=1) + result[BINS:, LANES:]
            both = jnp.where(low_half, first, second).T
            out_ref[2 * pair] = both[:half]
            out_ref[2 * pair + 1] = both[half:]
            return carry

        lax.fori_loop(0, TRIAL_BLOCK // 2, one_pair, 0, unroll=2)


def dedisperse(series, phases, forward, inverse, beams):
    freqs, trials, width = phases.shape
    channels = width // 4
    pieces = len(series)
    freq_steps = freqs // FREQ_BLOCK
    trial_steps = trials // TRIAL_BLOCK
    series = [piece.reshape(-1, 2 * beams, BINS) for piece in series]
    whole = [
        pl.BlockSpec(piece.shape, lambda g: (0, 0, 0), pipeline_mode=pl.Buffered(1))
        for piece in series
    ]
    return pl.pallas_call(
        lambda *refs: dedisperse_kernel(pieces, channels, trials, freq_steps, *refs),
        out_shape=jax.ShapeDtypeStruct((trials, beams, BINS), jnp.float32),
        grid=(freq_steps + trial_steps,),
        in_specs=whole
        + [
            pl.BlockSpec(
                (FREQ_BLOCK, trials, width),
                lambda g: (jnp.minimum(g, freq_steps - 1), 0, 0),
            ),
            pl.BlockSpec(forward.shape, lambda g: (0, 0)),
            pl.BlockSpec(inverse.shape, lambda g: (0, 0)),
        ],
        out_specs=pl.BlockSpec(
            (TRIAL_BLOCK, beams, BINS), lambda g: (jnp.maximum(g - freq_steps, 0), 0, 0)
        ),
        scratch_shapes=[
            pltpu.VMEM((FREQ_ROWS * channels, LANES), jnp.float32),
            pltpu.VMEM((trials * FREQ_ROWS, LANES), jnp.float32),
        ],
        compiler_params=pltpu.CompilerParams(vmem_limit_bytes=VMEM_LIMIT),
        cost_estimate=pl.CostEstimate(
            flops=freqs * trials * 6 * channels * LANES * 2 * 4,
            bytes_accessed=phases.size * 2 + trials * beams * BINS * 4,
            transcendentals=0,
        ),
        name="dedisperse",
    )(*series, phases, forward, inverse)


def shards_wide(voltages, prototype, beam_weights, input_order, beam_order, trial_delays):
    owners = lax.axis_size("section") * lax.axis_size("sub")
    chan_dev, _, beams, inputs = beam_weights.shape
    local_inputs = voltages.shape[0]
    trials = trial_delays.shape[0]
    cuts = sorted({0, chan_dev // 8, chan_dev // 2, chan_dev})
    parts = list(zip(cuts[:-1], cuts[1:]))

    turned_volts = jnp.transpose(voltages, (1, 0, 2)).reshape(2 * local_inputs, -1)
    bank = filter_matrix(prototype)[0].reshape(owners, chan_dev, 2, TAPS * LANES)
    bank = jnp.transpose(bank, (2, 0, 1, 3))
    input_pick = (
        input_order[:, None] == jnp.arange(inputs, dtype=jnp.int32)[None, :]
    ).astype(jnp.bfloat16)
    beam_pick = (
        beam_order[:, None] == jnp.arange(beams, dtype=jnp.int32)[None, :]
    ).astype(jnp.bfloat16)
    delays = trial_delays.reshape(trials, owners, chan_dev)

    def exchange(piece):
        return lax.all_to_all(piece, OWNER_AXES, split_axis=0, concat_axis=0, tiled=True)

    def spectra_of(low, high):
        rows = bank[:, :, low:high].reshape(-1, TAPS * LANES)
        return channelize_chunk(turned_volts, rows, owners, high - low)

    def weights_of(low, high):
        return jnp.einsum(
            "ip,cqbp->cqib",
            input_pick,
            beam_weights[low:high],
            preferred_element_type=jnp.float32,
        ).astype(jnp.bfloat16)

    def beams_of(arrived, weights):
        spectra = arrived.reshape(owners, -1, SPECTRA, 2 * local_inputs)
        return beam_chunk(spectra, weights, beam_pick, owners)

    split = parts[-1][0]
    delays = jnp.concatenate(
        [delays[:, :, :split].reshape(trials, -1), delays[:, :, split:].reshape(trials, -1)], axis=1
    )
    phases = phase_table(delays)

    arrived, weights, outgoing = [], [], []
    for step, (low, high) in enumerate(parts):
        piece = spectra_of(low, high)
        if step >= 2:
            outgoing.append(beams_of(arrived[step - 2], weights[step - 2]))
            outgoing[-1], piece = lax.optimization_barrier((outgoing[-1], piece))
        if step == len(parts) - 1:
            phases, piece = lax.optimization_barrier((phases, piece))
        weights.append(weights_of(low, high))
        arrived.append(exchange(piece))
    if len(parts) >= 2:
        outgoing.append(beams_of(arrived[-2], weights[-2]))
        early = outgoing[0] if len(outgoing) == 1 else jnp.concatenate(outgoing, axis=1)
        early, weights[-1], arrived[-1] = lax.optimization_barrier((early, weights[-1], arrived[-1]))
        series = [exchange(early)]
    else:
        series = []
    series.append(exchange(beams_of(arrived[-1], weights[-1])))
    return dedisperse(series, phases, forward_table(), inverse_table(), beams // owners)


def channelize(block_volts, matrix):
    input_count = block_volts.shape[0]
    frames = block_volts.reshape(input_count, 2, SPECTRA + TAPS - 1, CHANS)
    windows = jnp.concatenate(
        [
            frames[:, part_index, tap_index : tap_index + SPECTRA, :]
            for part_index in range(2)
            for tap_index in range(TAPS)
        ],
        axis=2,
    )
    result = lax.dot_general(
        matrix, windows, (((2,), (2,)), ((), ())), preferred_element_type=jnp.float32
    )
    return result.astype(jnp.bfloat16)


def fold_time(series):
    shape_head = series.shape[:-1]
    return series.reshape(shape_head + (series.shape[-1] // DOWN, DOWN)).sum(axis=-1)


def shards_narrow(voltages, prototype, beam_weights, input_order, beam_order, trial_delays):
    section_count = lax.axis_size("section")
    sub_count = lax.axis_size("sub")
    owners = section_count * sub_count
    chan_dev = CHANS // owners
    beam_dev = BEAMS // owners
    input_rows = jnp.arange(INPUTS, dtype=jnp.int32)
    channel_rows = jnp.arange(CHANS, dtype=jnp.int32)
    spectra_local = channelize(voltages, filter_matrix(prototype))
    physical = jnp.take(input_order, input_rows)
    position_of = (
        jnp.zeros((INPUTS,), jnp.int32).at[physical].set(jnp.arange(INPUTS, dtype=jnp.int32))
    )
    weight_real = beam_weights[:, 0]
    weight_imag = beam_weights[:, 1]
    ordered = jnp.take(
        lax.all_to_all(spectra_local, ("section", "sub"), split_axis=1, concat_axis=2, tiled=True),
        position_of,
        axis=2,
    )
    with_real = jnp.einsum(
        "cbi,pcit->pcbt", weight_real, ordered, preferred_element_type=jnp.float32
    )
    with_imag = jnp.einsum(
        "cbi,pcit->pcbt", weight_imag, ordered, preferred_element_type=jnp.float32
    )
    beam_real = with_real[0] - with_imag[1]
    beam_imag = with_real[1] + with_imag[0]
    power = beam_real * beam_real + beam_imag * beam_imag
    power = jnp.take(power, beam_order, axis=1)
    outgoing = fold_time(power)
    outgoing = outgoing.reshape(chan_dev, owners, beam_dev, outgoing.shape[2])
    half = BINS // 2 + 1
    delay_table = jnp.transpose(jnp.take(trial_delays, channel_rows, axis=1))
    sample_index = jnp.arange(BINS, dtype=jnp.int32)
    freq_index = jnp.arange(half, dtype=jnp.int32)
    half_angles = (
        2.0
        * math.pi
        / BINS
        * (freq_index[:, None] * sample_index[None, :] % BINS).astype(jnp.float32)
    )
    forward_cos = jnp.cos(half_angles)
    forward_sin = -jnp.sin(half_angles)
    edge = (freq_index == 0) | (freq_index == BINS // 2)
    fold_weight = (jnp.where(edge, 1.0, 2.0) / BINS).astype(jnp.float32)[:, None]
    inverse_cos = fold_weight * forward_cos
    inverse_sin = fold_weight * forward_sin
    twiddle_angles = (
        2.0
        * math.pi
        / BINS
        * (sample_index[:, None] * freq_index[None, :] % BINS).astype(jnp.float32)
    )
    twiddle = jnp.concatenate([jnp.cos(twiddle_angles), jnp.sin(twiddle_angles)], axis=1)
    twiddle_high = twiddle.astype(jnp.bfloat16)
    twiddle_low = (twiddle - twiddle_high.astype(jnp.float32)).astype(jnp.bfloat16)
    one_hot = (delay_table[:, :, None] == sample_index[None, None, :]).astype(jnp.bfloat16)
    phase_grid = jnp.einsum(
        "cdv,vf->cdf", one_hot, twiddle_high, preferred_element_type=jnp.float32
    ) + jnp.einsum("cdv,vf->cdf", one_hot, twiddle_low, preferred_element_type=jnp.float32)
    cos_grid = phase_grid[:, :, :half]
    sin_grid = phase_grid[:, :, half:]
    highest = lax.Precision.HIGHEST
    series = lax.all_to_all(outgoing, ("section", "sub"), split_axis=1, concat_axis=0, tiled=True)[
        :, 0
    ]
    centred = series - jnp.mean(series, axis=2, keepdims=True)
    spread = jnp.mean(centred * centred, axis=2, keepdims=True)
    normed = centred / jnp.sqrt(spread + 1e-06)
    spec_real = jnp.einsum("cbu,fu->fbc", normed, forward_cos, precision=highest)
    spec_imag = jnp.einsum("cbu,fu->fbc", normed, forward_sin, precision=highest)
    out_real = jnp.einsum("fbc,cdf->fbd", spec_real, cos_grid, precision=highest) - jnp.einsum(
        "fbc,cdf->fbd", spec_imag, sin_grid, precision=highest
    )
    out_imag = jnp.einsum("fbc,cdf->fbd", spec_real, sin_grid, precision=highest) + jnp.einsum(
        "fbc,cdf->fbd", spec_imag, cos_grid, precision=highest
    )
    result = jnp.einsum("fbd,fu->dbu", out_real, inverse_cos, precision=highest) + jnp.einsum(
        "fbd,fu->dbu", out_imag, inverse_sin, precision=highest
    )
    return result / math.sqrt(CHANS)


def solution(mesh):
    owners = mesh.shape["section"] * mesh.shape["sub"]
    wide = 2 * (INPUTS // owners) == LANES

    return jax.shard_map(
        shards_wide if wide else shards_narrow,
        mesh=mesh,
        in_specs=(
            P(("groups", "section", "sub"), None, None),
            P(),
            P(("groups", "section", "sub"), None, None, None),
            P(),
            P(),
            P(),
        ),
        out_specs=P(None, ("groups", "section", "sub"), None),
        check_vma=False,
    )
```
